32 devices in a mesh: region: 8 (over y, x, core), band: 4 (over z).
Axes of the slice: x: 2, y: 2, z: 4, core: 2. Of those that a mesh axis runs over, the one named last changes fastest.
Arguments:
- anomalies: bfloat16 [524288, 128], P(('region', 'band')), may hold values from -28 to 28
- operator: bfloat16 [512, 4, 128, 128], P(('region', 'band')), may hold values from -0.0029296875 to 0.0029296875
- local_tile_index: int32 [512, 4], P(('region', 'band')), may hold values from 0 to 127
- err_std: float32 [65536], P(('region', 'band')), may hold values from 3 to 58
- err_corr: float32 [65536], P(('region', 'band')), may hold values from -1 to 1
Outputs:
- whitened: float32 [65536, 128], P(('region', 'band'))
- updated: bfloat16 [524288, 128], P(('region', 'band'))
The draws below stay inside these ranges and needn't reach their ends.
Inputs may be any that keep to these rules, and one draw needn't show every extreme that they name: `local_tile_index`: entry [j, k] names a tile of the device that lies k places further along band, cyclically, in the region of the device that holds block j.
All inputs are finite; a program needn't handle non-finite values.
Results may differ from the reference program's by a relative error of at most 0.0043.
The reference program's roundings to bfloat16 on the way (of `transform`) count: a program that leaves them out, or rounds other values in their place, can miss the bound.
Values may be sent and summed in bfloat16 or wider, within the bound.
No kernel may reach another device: no remote copies, remote signals or barrier semaphores. Data moves between devices by JAX's collectives and lax.ppermute only.
A program may use at most 64 MiB of HBM per device.

```python
import math
import jax
import jax.numpy as jnp
from jax import lax

M = 128
TILE = 128
TILES_DEV = 128
BLK_DEV = 16
NODES = 524288
OBS_BLOCKS = 512
NOBS = 65536
N_BAND = 4


def draw_anomalies(key, part):
    keys = jax.random.split(jax.random.fold_in(key, 11), 4)
    noise = jnp.clip(jax.random.normal(keys[0], (NODES, M), jnp.float32), -4.0, 4.0)
    common_weight = 0.5
    member_scale = jnp.exp(jax.random.uniform(keys[1], (1, M), jnp.float32, math.log(0.5), math.log(2.0)))
    node_factors = jnp.clip(jax.random.normal(keys[2], (NODES, 3), jnp.float32), -3.0, 3.0)
    member_factors = jnp.clip(jax.random.normal(keys[3], (3, M), jnp.float32), -3.0, 3.0)
    common = node_factors[:, 0:1] * member_factors[0:1, :]
    common = common + node_factors[:, 1:2] * member_factors[1:2, :]
    common = common + node_factors[:, 2:3] * member_factors[2:3, :]
    return (noise * member_scale + common_weight * common).astype(jnp.bfloat16)


def draw_err_std(key, part):
    keys = jax.random.split(jax.random.fold_in(key, 23), 1)
    position = jnp.arange(NOBS, dtype=jnp.float32) / max(NOBS - 1, 1)
    base = jnp.exp(jax.random.uniform(keys[0], (NOBS,), jnp.float32, math.log(3.0), math.log(18.0)))
    trend = jnp.exp((1.0 - position) * math.log(1.8))
    return (base * trend).astype(jnp.float32)


def draw_err_corr(key, part):
    keys = jax.random.split(jax.random.fold_in(key, 37), 4)
    levels = NOBS // TILE
    level_rate = jnp.exp(jax.random.uniform(keys[0], (levels,), jnp.float32, math.log(0.5), math.log(2.0)))
    keep_low = 0.62
    rate = jnp.repeat(level_rate, TILE)
    absolute_size = 1.0 - rate * (0.7 / NOBS)
    spots = jax.random.randint(keys[1], (3,), 0, NOBS)
    retained_flags = jax.random.uniform(keys[2], (3,), jnp.float32, keep_low, 0.8)
    position = jnp.arange(NOBS, dtype=jnp.int32)
    match_found = position[:, None] == spots[None, :]
    sudden_jump = jnp.prod(jnp.where(match_found, retained_flags[None, :], 1.0), axis=1)
    sign_pattern = jnp.where(jax.random.bernoulli(keys[3], 0.5, (NOBS,)), 1.0, -1.0)
    return (sign_pattern * absolute_size * sudden_jump).astype(jnp.float32)


def plant(result, stream_key, smallest, top_value):
    place = [jax.random.randint(jax.random.fold_in(stream_key, axis), (), 0, length) for axis, length in enumerate(result.shape)]
    longest = result.shape.index(max(result.shape))
    neighbour = place[:longest] + [(place[longest] + 1) % result.shape[longest]] + place[longest + 1:]
    return result.at[tuple(place)].set(smallest).at[tuple(neighbour)].set(top_value)


def steps_of(own_key, extent, cuts, smallest, top_value):
    def one(dim, shards_of):
        steps = jax.random.uniform(jax.random.fold_in(jax.random.fold_in(own_key, 6), dim), (shards_of,), jnp.float32, smallest / len(cuts), top_value / len(cuts))
        return jnp.repeat(jnp.exp(steps), extent[dim] // shards_of).reshape((-1,) + (1,) * (len(extent) - dim - 1))

    gain = one(*cuts[0])
    for cut in cuts[1:]:
        gain = gain * one(*cut)
    return gain


def gaussian(rng, shape, width, reach, shards=(), kind=jnp.bfloat16):
    result = jax.random.normal(rng, shape, jnp.float32) * width
    if len(shards) > 0:
        result = steps_of(rng, shape, shards, -0.22, 0.18) * result
    return jnp.clip(result, min=-reach, max=reach).astype(kind)


def setup_inputs(seed: int = 0) -> dict:
    seeds = jax.random.split(jax.random.key(seed), 6)
    anomalies = draw_anomalies(jax.random.fold_in(seeds[5], 71), 0)
    operator = gaussian(seeds[1], (OBS_BLOCKS, N_BAND, TILE, TILE), (N_BAND * TILE * NOBS // 8) ** -0.5, 0.0029296875, ((0, 32),))
    local_tile_index = plant(jax.random.randint(seeds[2], (OBS_BLOCKS, N_BAND), 0, TILES_DEV), jax.random.fold_in(seeds[2], 1), 0, TILES_DEV - 1).astype(jnp.int32)
    err_std = draw_err_std(jax.random.fold_in(seeds[5], 71), 0)
    err_corr = draw_err_corr(jax.random.fold_in(seeds[5], 71), 0)
    return dict(anomalies=anomalies, operator=operator, local_tile_index=local_tile_index, err_std=err_std, err_corr=err_corr)


def affine_link(earlier, trailing):
    return (earlier[0] * trailing[0], trailing[0] * earlier[1] + trailing[1])

def reference(anomalies, operator, local_tile_index, err_std, err_corr):
    members = anomalies.shape[1]
    groups = OBS_BLOCKS // BLK_DEV
    tiles_all = anomalies.reshape(-1, TILE, members)
    block_ids = jnp.arange(OBS_BLOCKS, dtype=jnp.int32)
    holder = block_ids // BLK_DEV
    region_of = holder // N_BAND
    band_of = holder % N_BAND
    offsets = jnp.arange(N_BAND, dtype=jnp.int32)
    target = region_of[:, None] * N_BAND + (band_of[:, None] + offsets[None, :]) % N_BAND
    node_tile = (target * TILES_DEV + local_tile_index.astype(jnp.int32)).astype(jnp.int32)

    def single_cluster(group_pair):
        op_blocks, tile_picks = group_pair
        picked = jnp.take(tiles_all, tile_picks, axis=0).astype(jnp.float32)
        return jnp.einsum('jkon,jknm->jom', op_blocks.astype(jnp.float32), picked, precision=lax.Precision.HIGHEST)
    predicted = lax.map(single_cluster, (operator.reshape(groups, BLK_DEV, N_BAND, TILE, TILE), node_tile.reshape(groups, BLK_DEV, N_BAND)))
    predicted = predicted.reshape(-1, members)
    rescaled_values = predicted / err_std[:, None]
    decay_coef = err_corr[:, None]
    _, whitened = lax.associative_scan(affine_link, (decay_coef, rescaled_values), axis=0)
    gram_total = (members - 1.0) * jnp.eye(members, dtype=jnp.float32) + jnp.dot(whitened.T.astype(jnp.float32), whitened.astype(jnp.float32), precision=lax.Precision.HIGHEST, preferred_element_type=jnp.float32)
    lower_factor = jnp.linalg.cholesky(gram_total)
    inverse = lax.linalg.triangular_solve(lower_factor, jnp.eye(members, dtype=jnp.float32), left_side=True, lower=True, transpose_a=True)
    transform = (math.sqrt(members - 1.0) * inverse).astype(jnp.bfloat16)

    def update(row_block):
        return jnp.dot(row_block.astype(jnp.float32), transform.astype(jnp.float32), preferred_element_type=jnp.float32).astype(jnp.bfloat16)
    updated = lax.map(update, anomalies.reshape(groups, -1, members)).reshape(-1, members)
    return (whitened, updated)
```

```python
import functools
import math

import jax
import jax.numpy as jnp
from jax import lax
from jax.experimental import pallas as pl
from jax.experimental.pallas import tpu as pltpu
from jax.sharding import PartitionSpec as P

SLOT = 8
f32, bf16 = jnp.float32, jnp.bfloat16


def shifted(block, axis, distance):
    n = lax.axis_size(axis)
    return lax.ppermute(block, axis, [((i + distance) % n, i) for i in range(n)])


def swapped(block, axis, mask):
    n = lax.axis_size(axis)
    return lax.ppermute(block, axis, [(i ^ mask, i) for i in range(n)])


def call(kernel, **kw):
    return pl.pallas_call(kernel, name=kernel.__name__, **kw)


ANY = pl.BlockSpec(memory_space=pl.ANY)
SMEM = pl.BlockSpec(memory_space=pltpu.SMEM)
VMEM = pl.BlockSpec(memory_space=pltpu.VMEM)


def gather(tiles, picks):
    count = picks.shape[0]

    def gather_tiles(picks_ref, tiles_ref, out_ref, sems):
        copies = [
            pltpu.make_async_copy(tiles_ref.at[picks_ref[j]], out_ref.at[j], sems.at[j])
            for j in range(count)
        ]
        for c in copies:
            c.start()
        for c in copies:
            c.wait()

    return pl.pallas_call(
        gather_tiles,
        name="gather_tiles",
        out_shape=jax.ShapeDtypeStruct((count,) + tiles.shape[1:], tiles.dtype),
        in_specs=[SMEM, ANY],
        out_specs=ANY,
        scratch_shapes=[pltpu.SemaphoreType.DMA((count,))],
    )(picks, tiles)


def split3(x):
    a = x.astype(bf16)
    r = x - a.astype(f32)
    b = r.astype(bf16)
    c = (r - b.astype(f32)).astype(bf16)
    return a, b, c


def weights(operator, err_std, err_corr):
    blocks, parts, tile, _ = operator.shape

    def weigh(op_ref, std_ref, corr_ref, w_ref, p_ref):
        rows = lax.broadcasted_iota(jnp.int32, (tile, tile), 0)
        cols = lax.broadcasted_iota(jnp.int32, (tile, tile), 1)
        prod = jnp.broadcast_to(corr_ref[0], (tile, tile)).T
        tri = jnp.where(rows == cols, 1.0, 0.0).astype(f32)
        d = 1
        while d < tile:
            keep = rows >= d
            tri = tri + prod * jnp.where(keep, pltpu.roll(tri, d, 0), 0.0)
            prod = prod * jnp.where(keep, pltpu.roll(prod, d, 0), 1.0)
            d *= 2
        scaled = tri * (1.0 / std_ref[0])
        op = jnp.concatenate([op_ref[0, k] for k in range(parts)], axis=1)
        w = sum(jnp.dot(t, op, preferred_element_type=f32) for t in split3(scaled)[::-1])
        high = w.astype(bf16)
        w_ref[0, 0:tile, :] = high
        w_ref[0, tile : 2 * tile, :] = (w - high.astype(f32)).astype(bf16)
        p_ref[0] = prod

    return call(
        weigh,
        grid=(blocks,),
        out_shape=(
            jax.ShapeDtypeStruct((blocks, 2 * tile, parts * tile), bf16),
            jax.ShapeDtypeStruct((blocks, tile, tile), f32),
        ),
        in_specs=[
            pl.BlockSpec((1, parts, tile, tile), lambda j: (j, 0, 0, 0)),
            pl.BlockSpec((1, 1, tile), lambda j: (j, 0, 0)),
            pl.BlockSpec((1, 1, tile), lambda j: (j, 0, 0)),
        ],
        out_specs=(
            pl.BlockSpec((1, 2 * tile, parts * tile), lambda j: (j, 0, 0)),
            pl.BlockSpec((1, tile, tile), lambda j: (j, 0, 0)),
        ),
    )(operator, err_std.reshape(blocks, 1, tile), err_corr.reshape(blocks, 1, tile))


def whiten(w, prods, picked, group):
    blocks, _, depth = w.shape
    tile, members = picked[0].shape[1:]
    parts = len(picked)

    def whiten_blocks(w_ref, p_ref, *refs):
        x_refs, (y_ref, a_ref, msg_ref, z, gram, state, decay, usum, ssum) = refs[:parts], refs[parts:]
        step = pl.program_id(0)

        @pl.when(step == 0)
        def _():
            gram[...] = jnp.zeros_like(gram)
            state[...] = jnp.zeros_like(state)
            decay[...] = jnp.ones_like(decay)
            usum[...] = jnp.zeros_like(usum)
            ssum[...] = jnp.zeros_like(ssum)

        carry, run = state[...], decay[...]
        u, s = usum[...], ssum[...]
        for j in range(group):
            x = jnp.concatenate([r[j] for r in x_refs], axis=0)
            both = jnp.dot(w_ref[j], x, preferred_element_type=f32)
            y = both[:tile] + both[tile:]
            y = y + p_ref[j] * carry[0:1]
            a = p_ref[j] * run[0:1]
            carry, run = y[tile - 8 :][7:8], a[tile - 8 :][7:8]
            y_ref[j] = y
            a_ref[j] = a
            u = u + jnp.sum((a * y).reshape(tile // 8, 8, members), axis=0)
            s = s + jnp.sum((a * a).reshape(tile // 8, 8, members), axis=0)
            high = y.astype(bf16)
            z[j * tile : (j + 1) * tile, 0:members] = high
            z[j * tile : (j + 1) * tile, members:] = (y - high.astype(f32)).astype(bf16)
        gram[...] += lax.dot_general(
            z[...], z[...], (((0,), (0,)), ((), ())), preferred_element_type=f32
        )
        state[...] = jnp.broadcast_to(carry, state.shape)
        decay[...] = jnp.broadcast_to(run, decay.shape)
        usum[...] = u
        ssum[...] = s

        @pl.when(step == pl.num_programs(0) - 1)
        def _():
            msg_ref[0:members] = (
                gram[0:members, 0:members]
                + (gram[0:members, members:] + gram[members:, 0:members])
                + gram[members:, members:]
            )
            zero = jnp.zeros((SLOT - 4, members), f32)
            msg_ref[members : members + SLOT] = jnp.concatenate(
                [carry, jnp.sum(u, 0, keepdims=True), run, jnp.sum(s, 0, keepdims=True), zero], axis=0
            )

    rows = pl.BlockSpec((group, tile, members), lambda i: (i, 0, 0))
    return call(
        whiten_blocks,
        grid=(blocks // group,),
        out_shape=(
            jax.ShapeDtypeStruct((blocks, tile, members), f32),
            jax.ShapeDtypeStruct((blocks, tile, members), f32),
            jax.ShapeDtypeStruct((members + SLOT, members), f32),
        ),
        in_specs=[pl.BlockSpec((group, 2 * tile, depth), lambda i: (i, 0, 0)), rows] + [rows] * parts,
        out_specs=(rows, rows, pl.BlockSpec((members + SLOT, members), lambda i: (0, 0))),
        scratch_shapes=[
            pltpu.VMEM((group * tile, 2 * members), bf16),
            pltpu.VMEM((2 * members, 2 * members), f32),
        ]
        + [pltpu.VMEM((8, members), f32)] * 4,
    )(w, prods, *picked)


def joined(messages, members):
    slots = messages[0].shape[0] - members

    def join(*refs):
        ins, out = refs[:-1], refs[-1]
        total = ins[0][0:members]
        for r in ins[1:]:
            total = total + r[0:members]
        out[0:members] = total
        for i, r in enumerate(ins):
            out[members + i * slots : members + (i + 1) * slots] = r[members:]

    return call(
        join,
        out_shape=jax.ShapeDtypeStruct((members + slots * len(messages), members), f32),
        in_specs=[VMEM] * len(messages),
        out_specs=VMEM,
    )(*messages)


def finish(message, y, decays, place, slots, devices):
    members = message.shape[1]
    blocks = y.shape[0]

    def settle(place_ref, slot_ref, msg_ref, y_ref, a_ref, w_ref, g_ref, left, right):
        place = place_ref[0]

        def one(d, c):
            slot = slot_ref[lax.bitwise_xor(d, place)]
            at = pl.multiple_of(members + slot * SLOT, SLOT)
            small = msg_ref[pl.ds(at, SLOT), :]
            v = small[1:2] + (0.5 * small[3:4]) * c
            left[pl.ds(d, 1), :] = v
            left[pl.ds(devices + d, 1), :] = c
            right[pl.ds(d, 1), :] = c
            right[pl.ds(devices + d, 1), :] = v
            return small[2:3] * c + small[0:1]

        lax.fori_loop(0, devices, one, jnp.zeros((1, members), f32))
        mine = right[pl.ds(place, 1), :]
        rows = lax.broadcasted_iota(jnp.int32, (members, members), 0)
        cols = lax.broadcasted_iota(jnp.int32, (members, members), 1)
        g_ref[...] = (
            msg_ref[0:members]
            + lax.dot_general(
                left[...], right[...], (((0,), (0,)), ((), ())),
                precision=lax.Precision.HIGHEST, preferred_element_type=f32,
            )
            + jnp.where(rows == cols, members - 1.0, 0.0)
        )
        for j in range(blocks):
            w_ref[j] = y_ref[j] + a_ref[j] * mine

    return call(
        settle,
        out_shape=(
            jax.ShapeDtypeStruct(y.shape, f32),
            jax.ShapeDtypeStruct((members, members), f32),
        ),
        in_specs=[SMEM, SMEM, VMEM, VMEM, VMEM],
        out_specs=(VMEM, VMEM),
        scratch_shapes=[pltpu.VMEM((2 * devices, members), f32)] * 2,
    )(place, slots, message, y, decays)


def local(anomalies, operator, local_tile_index, err_std, err_corr):
    members = anomalies.shape[1]
    tile = operator.shape[2]
    blocks = operator.shape[0]
    bands, regions = lax.axis_size("band"), lax.axis_size("region")
    devices = regions * bands
    place = (lax.axis_index("region") * bands + lax.axis_index("band")).astype(jnp.int32).reshape(1)
    tiles = anomalies.reshape(-1, tile, members)

    asked = [shifted(local_tile_index[:, k], "band", bands - k) for k in range(1, bands)]
    picked = [gather(tiles, local_tile_index[:, 0])]
    for k in range(1, bands):
        picked.append(shifted(gather(tiles, asked[k - 1]), "band", k))

    w, prods = weights(operator, err_std, err_corr)
    y, decays, message = whiten(w, prods, picked, 4)

    masks = [("band", list(range(1, bands)))]
    bit = 2
    while bit < regions:
        masks.append(("region", [bit, 2 * bit, 3 * bit] if 2 * bit < regions else [bit]))
        bit *= 4
    masks.append(("region", [1]))
    order = [0]
    for axis, group in masks:
        message = joined([message] + [swapped(message, axis, m) for m in group], members)
        unit = bands if axis == "region" else 1
        order = [o ^ (m * unit) for m in [0] + group for o in order]
    slots = jnp.array([order.index(t) for t in range(devices)], jnp.int32)

    whitened, gram = finish(message, y, decays, place, slots, devices)
    lower_factor = jnp.linalg.cholesky(gram)
    inverse = lax.linalg.triangular_solve(
        lower_factor, jnp.eye(members, dtype=f32), left_side=True, lower=True, transpose_a=True
    )
    transform = (math.sqrt(members - 1.0) * inverse).astype(bf16)
    updated = jnp.dot(anomalies, transform, preferred_element_type=f32).astype(bf16)
    return whitened.reshape(-1, members), updated


def solution(mesh):
    both = ("region", "band")
    placed = (P(both, None), P(both, None, None, None), P(both, None), P(both), P(both))
    return jax.shard_map(
        local, mesh=mesh, in_specs=placed, out_specs=(P(both, None), P(both, None)), check_vma=False
    )
```

```python
import functools
import math

import jax
import jax.numpy as jnp
from jax import lax
from jax.experimental import pallas as pl
from jax.experimental.pallas import tpu as pltpu
from jax.sharding import PartitionSpec as P

SLOT = 8
GRANT = 24 << 20
f32, bf16 = jnp.float32, jnp.bfloat16


def shifted(block, axis, distance):
    n = lax.axis_size(axis)
    return lax.ppermute(block, axis, [((i + distance) % n, i) for i in range(n)])


def swapped(block, axis, mask):
    n = lax.axis_size(axis)
    return lax.ppermute(block, axis, [(i ^ mask, i) for i in range(n)])


def call(kernel, **kw):
    limits = pltpu.CompilerParams(vmem_limit_bytes=GRANT)
    return pl.pallas_call(kernel, name=kernel.__name__, compiler_params=limits, **kw)


def near(x):
    return pltpu.with_memory_space_constraint(x, pltpu.VMEM)


def near_out(shape, dtype):
    return pltpu.VMEM(shape, dtype)


ANY = pl.BlockSpec(memory_space=pl.ANY)
SMEM = pl.BlockSpec(memory_space=pltpu.SMEM)
VMEM = pl.BlockSpec(memory_space=pltpu.VMEM)


def gather(tiles, picks):
    count = picks.shape[0]

    def gather_tiles(picks_ref, tiles_ref, out_ref, sems):
        copies = [
            pltpu.make_async_copy(tiles_ref.at[picks_ref[j]], out_ref.at[j], sems.at[j])
            for j in range(count)
        ]
        for c in copies:
            c.start()
        for c in copies:
            c.wait()

    return call(
        gather_tiles,
        out_shape=near_out((count,) + tiles.shape[1:], tiles.dtype),
        in_specs=[SMEM, ANY],
        out_specs=VMEM,
        scratch_shapes=[pltpu.SemaphoreType.DMA((count,))],
    )(picks, tiles)


def split3(x):
    a = x.astype(bf16)
    r = x - a.astype(f32)
    b = r.astype(bf16)
    c = (r - b.astype(f32)).astype(bf16)
    return a, b, c


def weights(operator, err_std, err_corr):
    blocks, parts, tile, _ = operator.shape

    def weigh(op_ref, std_ref, corr_ref, w_ref, p_ref):
        rows = lax.broadcasted_iota(jnp.int32, (tile, tile), 0)
        cols = lax.broadcasted_iota(jnp.int32, (tile, tile), 1)

        def one(j, _):
            prod = jnp.broadcast_to(corr_ref[j], (tile, tile)).T
            tri = jnp.where(rows == cols, 1.0, 0.0).astype(f32)
            d = 1
            while d < tile:
                keep = rows >= d
                tri = tri + prod * jnp.where(keep, pltpu.roll(tri, d, 0), 0.0)
                prod = prod * jnp.where(keep, pltpu.roll(prod, d, 0), 1.0)
                d *= 2
            scaled = tri * (1.0 / std_ref[j])
            op = jnp.concatenate([op_ref[j, k] for k in range(parts)], axis=1)
            w = sum(jnp.dot(t, op, preferred_element_type=f32) for t in split3(scaled)[::-1])
            high = w.astype(bf16)
            w_ref[j, 0:tile, :] = high
            w_ref[j, tile : 2 * tile, :] = (w - high.astype(f32)).astype(bf16)
            p_ref[j] = prod
            return 0

        lax.fori_loop(0, blocks, one, 0)

    return call(
        weigh,
        out_shape=(
            near_out((blocks, 2 * tile, parts * tile), bf16),
            near_out((blocks, tile, tile), f32),
        ),
        in_specs=[VMEM] * 3,
        out_specs=(VMEM, VMEM),
    )(operator, err_std.reshape(blocks, 1, tile), err_corr.reshape(blocks, 1, tile))


def whiten(w, prods, picked, group):
    blocks, _, depth = w.shape
    tile, members = picked[0].shape[1:]
    parts = len(picked)

    def whiten_blocks(w_ref, p_ref, *refs):
        x_refs, (y_ref, a_ref, msg_ref, z, gram) = refs[:parts], refs[parts:]
        gram[...] = jnp.zeros_like(gram)

        def some(step, state):
            carry, run, u, s = state
            for i in range(group):
                j = step * group + i
                x = jnp.concatenate([r[j] for r in x_refs], axis=0)
                both = jnp.dot(w_ref[j], x, preferred_element_type=f32)
                y = both[:tile] + both[tile:]
                y = y + p_ref[j] * carry
                a = p_ref[j] * run
                carry, run = y[tile - 8 :][7:8], a[tile - 8 :][7:8]
                y_ref[j] = y
                a_ref[j] = a
                u = u + jnp.sum((a * y).reshape(tile // 8, 8, members), axis=0)
                s = s + jnp.sum((a * a).reshape(tile // 8, 8, members), axis=0)
                high = y.astype(bf16)
                z[i * tile : (i + 1) * tile, 0:members] = high
                z[i * tile : (i + 1) * tile, members:] = (y - high.astype(f32)).astype(bf16)
            gram[...] += lax.dot_general(
                z[...], z[...], (((0,), (0,)), ((), ())), preferred_element_type=f32
            )
            return carry, run, u, s

        row, sums = jnp.zeros((1, members), f32), jnp.zeros((8, members), f32)
        carry, run, u, s = lax.fori_loop(0, blocks // group, some, (row, row + 1.0, sums, sums))
        msg_ref[0:members] = (
            gram[0:members, 0:members]
            + (gram[0:members, members:] + gram[members:, 0:members])
            + gram[members:, members:]
        )
        zero = jnp.zeros((SLOT - 4, members), f32)
        msg_ref[members : members + SLOT] = jnp.concatenate(
            [carry, jnp.sum(u, 0, keepdims=True), run, jnp.sum(s, 0, keepdims=True), zero], axis=0
        )

    return call(
        whiten_blocks,
        out_shape=(
            near_out((blocks, tile, members), f32),
            near_out((blocks, tile, members), f32),
            near_out((members + SLOT, members), f32),
        ),
        in_specs=[VMEM] * (2 + parts),
        out_specs=(VMEM, VMEM, VMEM),
        scratch_shapes=[
            pltpu.VMEM((group * tile, 2 * members), bf16),
            pltpu.VMEM((2 * members, 2 * members), f32),
        ],
    )(near(w), near(prods), *[near(x) for x in picked])


def joined(messages, members):
    slots = messages[0].shape[0] - members

    def join(*refs):
        ins, out = refs[:-1], refs[-1]
        total = ins[0][0:members]
        for r in ins[1:]:
            total = total + r[0:members]
        out[0:members] = total
        for i, r in enumerate(ins):
            out[members + i * slots : members + (i + 1) * slots] = r[members:]

    return call(
        join,
        out_shape=near_out((members + slots * len(messages), members), f32),
        in_specs=[VMEM] * len(messages),
        out_specs=VMEM,
    )(*[near(m) for m in messages])


def finish(message, y, decays, place, slots, devices):
    members = message.shape[1]
    blocks = y.shape[0]

    def settle(place_ref, slot_ref, msg_ref, y_ref, a_ref, w_ref, g_ref, left, right):
        place = place_ref[0]

        def one(d, c):
            slot = slot_ref[lax.bitwise_xor(d, place)]
            at = pl.multiple_of(members + slot * SLOT, SLOT)
            small = msg_ref[pl.ds(at, SLOT), :]
            v = small[1:2] + (0.5 * small[3:4]) * c
            left[pl.ds(d, 1), :] = v
            left[pl.ds(devices + d, 1), :] = c
            right[pl.ds(d, 1), :] = c
            right[pl.ds(devices + d, 1), :] = v
            return small[2:3] * c + small[0:1]

        lax.fori_loop(0, devices, one, jnp.zeros((1, members), f32))
        mine = right[pl.ds(place, 1), :]
        rows = lax.broadcasted_iota(jnp.int32, (members, members), 0)
        cols = lax.broadcasted_iota(jnp.int32, (members, members), 1)
        g_ref[...] = (
            msg_ref[0:members]
            + lax.dot_general(
                left[...], right[...], (((0,), (0,)), ((), ())),
                precision=lax.Precision.HIGHEST, preferred_element_type=f32,
            )
            + jnp.where(rows == cols, members - 1.0, 0.0)
        )
        for j in range(blocks):
            w_ref[j] = y_ref[j] + a_ref[j] * mine

    return call(
        settle,
        out_shape=(
            jax.ShapeDtypeStruct(y.shape, f32),
            jax.ShapeDtypeStruct((members, members), f32),
        ),
        in_specs=[SMEM, SMEM, VMEM, VMEM, VMEM],
        out_specs=(VMEM, VMEM),
        scratch_shapes=[pltpu.VMEM((2 * devices, members), f32)] * 2,
    )(place, slots, near(message), near(y), near(decays))


def local(anomalies, operator, local_tile_index, err_std, err_corr):
    members = anomalies.shape[1]
    tile = operator.shape[2]
    blocks = operator.shape[0]
    bands, regions = lax.axis_size("band"), lax.axis_size("region")
    devices = regions * bands
    place = (lax.axis_index("region") * bands + lax.axis_index("band")).astype(jnp.int32).reshape(1)
    tiles = anomalies.reshape(-1, tile, members)

    asked = [shifted(local_tile_index[:, k], "band", bands - k) for k in range(1, bands)]
    picked = [gather(tiles, local_tile_index[:, 0])]
    for k in range(1, bands):
        picked.append(shifted(gather(tiles, asked[k - 1]), "band", k))

    w, prods = weights(operator, err_std, err_corr)
    y, decays, message = whiten(w, prods, picked, 4)

    masks = [("band", list(range(1, bands)))]
    bit = 2
    while bit < regions:
        masks.append(("region", [bit, 2 * bit, 3 * bit] if 2 * bit < regions else [bit]))
        bit *= 4
    masks.append(("region", [1]))
    order = [0]
    for axis, group in masks:
        message = joined([message] + [swapped(message, axis, m) for m in group], members)
        unit = bands if axis == "region" else 1
        order = [o ^ (m * unit) for m in [0] + group for o in order]
    slots = jnp.array([order.index(t) for t in range(devices)], jnp.int32)

    whitened, gram = finish(message, y, decays, place, slots, devices)
    lower_factor = jnp.linalg.cholesky(gram)
    inverse = lax.linalg.triangular_solve(
        lower_factor, jnp.eye(members, dtype=f32), left_side=True, lower=True, transpose_a=True
    )
    transform = (math.sqrt(members - 1.0) * inverse).astype(bf16)
    updated = jnp.dot(anomalies, transform, preferred_element_type=f32).astype(bf16)
    return whitened.reshape(-1, members), updated


def solution(mesh):
    both = ("region", "band")
    placed = (P(both, None), P(both, None, None, None), P(both, None), P(both), P(both))
    return jax.shard_map(
        local, mesh=mesh, in_specs=placed, out_specs=(P(both, None), P(both, None)), check_vma=False
    )
```

```python
import functools
import math

import jax
import jax.numpy as jnp
from jax import lax
from jax.experimental import pallas as pl
from jax.experimental.pallas import tpu as pltpu
from jax.sharding import PartitionSpec as P

SLOT = 8
GRANT = 24 << 20
f32, bf16 = jnp.float32, jnp.bfloat16


def shifted(block, axis, distance):
    n = lax.axis_size(axis)
    return lax.ppermute(block, axis, [((i + distance) % n, i) for i in range(n)])


def swapped(block, axis, mask):
    n = lax.axis_size(axis)
    return lax.ppermute(block, axis, [(i ^ mask, i) for i in range(n)])


def call(kernel, **kw):
    limits = pltpu.CompilerParams(vmem_limit_bytes=GRANT)
    return pl.pallas_call(kernel, name=kernel.__name__, compiler_params=limits, **kw)


def near(x):
    return pltpu.with_memory_space_constraint(x, pltpu.VMEM)


def near_out(shape, dtype):
    return pltpu.VMEM(shape, dtype)


ANY = pl.BlockSpec(memory_space=pl.ANY)
SMEM = pl.BlockSpec(memory_space=pltpu.SMEM)
VMEM = pl.BlockSpec(memory_space=pltpu.VMEM)


def gather(tiles, picks):
    count = picks.shape[0]

    def gather_tiles(picks_ref, tiles_ref, out_ref, sems):
        copies = [
            pltpu.make_async_copy(tiles_ref.at[picks_ref[j]], out_ref.at[j], sems.at[j])
            for j in range(count)
        ]
        for c in copies:
            c.start()
        for c in copies:
            c.wait()

    return call(
        gather_tiles,
        out_shape=near_out((count,) + tiles.shape[1:], tiles.dtype),
        in_specs=[SMEM, ANY],
        out_specs=VMEM,
        scratch_shapes=[pltpu.SemaphoreType.DMA((count,))],
    )(picks, tiles)


def split3(x):
    a = x.astype(bf16)
    r = x - a.astype(f32)
    b = r.astype(bf16)
    c = (r - b.astype(f32)).astype(bf16)
    return a, b, c


def weights(operator, err_std, err_corr):
    blocks, parts, tile, _ = operator.shape

    def weigh(op_ref, std_ref, corr_ref, w_ref, p_ref):
        rows = lax.broadcasted_iota(jnp.int32, (tile, tile), 0)
        cols = lax.broadcasted_iota(jnp.int32, (tile, tile), 1)

        def one(j, _):
            prod = jnp.broadcast_to(corr_ref[j], (tile, tile)).T
            tri = jnp.where(rows == cols, 1.0, 0.0).astype(f32)
            d = 1
            while d < tile:
                keep = rows >= d
                tri = tri + prod * jnp.where(keep, pltpu.roll(tri, d, 0), 0.0)
                prod = prod * jnp.where(keep, pltpu.roll(prod, d, 0), 1.0)
                d *= 2
            scaled = tri * (1.0 / std_ref[j])
            op = jnp.concatenate([op_ref[j, k] for k in range(parts)], axis=1)
            w = sum(jnp.dot(t, op, preferred_element_type=f32) for t in split3(scaled)[::-1])
            high = w.astype(bf16)
            w_ref[j, 0:tile, :] = high
            w_ref[j, tile : 2 * tile, :] = (w - high.astype(f32)).astype(bf16)
            p_ref[j] = prod
            return 0

        lax.fori_loop(0, blocks, one, 0)

    return call(
        weigh,
        out_shape=(
            near_out((blocks, 2 * tile, parts * tile), bf16),
            near_out((blocks, tile, tile), f32),
        ),
        in_specs=[VMEM] * 3,
        out_specs=(VMEM, VMEM),
    )(operator, err_std.reshape(blocks, 1, tile), err_corr.reshape(blocks, 1, tile))


def whiten(w, prods, picked, group):
    blocks, _, depth = w.shape
    tile, members = picked[0].shape[1:]
    parts = len(picked)

    def whiten_blocks(w_ref, p_ref, *refs):
        x_refs, (y_ref, a_ref, msg_ref, z, gram) = refs[:parts], refs[parts:]
        gram[...] = jnp.zeros_like(gram)

        def some(step, state):
            carry, run, u, s = state
            for i in range(group):
                j = step * group + i
                x = jnp.concatenate([r[j] for r in x_refs], axis=0)
                both = jnp.dot(w_ref[j], x, preferred_element_type=f32)
                y = both[:tile] + both[tile:]
                y = y + p_ref[j] * carry
                a = p_ref[j] * run
                carry, run = y[tile - 8 :][7:8], a[tile - 8 :][7:8]
                y_ref[j] = y
                a_ref[j] = a
                u = u + jnp.sum((a * y).reshape(tile // 8, 8, members), axis=0)
                s = s + jnp.sum((a * a).reshape(tile // 8, 8, members), axis=0)
                high = y.astype(bf16)
                z[i * tile : (i + 1) * tile, 0:members] = high
                z[i * tile : (i + 1) * tile, members:] = (y - high.astype(f32)).astype(bf16)
            gram[...] += lax.dot_general(
                z[...], z[...], (((0,), (0,)), ((), ())), preferred_element_type=f32
            )
            return carry, run, u, s

        row, sums = jnp.zeros((1, members), f32), jnp.zeros((8, members), f32)
        carry, run, u, s = lax.fori_loop(0, blocks // group, some, (row, row + 1.0, sums, sums))
        msg_ref[0:members] = (
            gram[0:members, 0:members]
            + (gram[0:members, members:] + gram[members:, 0:members])
            + gram[members:, members:]
        )
        zero = jnp.zeros((SLOT - 4, members), f32)
        msg_ref[members : members + SLOT] = jnp.concatenate(
            [carry, jnp.sum(u, 0, keepdims=True), run, jnp.sum(s, 0, keepdims=True), zero], axis=0
        )

    return call(
        whiten_blocks,
        out_shape=(
            near_out((blocks, tile, members), f32),
            near_out((blocks, tile, members), f32),
            near_out((members + SLOT, members), f32),
        ),
        in_specs=[VMEM] * (2 + parts),
        out_specs=(VMEM, VMEM, VMEM),
        scratch_shapes=[
            pltpu.VMEM((group * tile, 2 * members), bf16),
            pltpu.VMEM((2 * members, 2 * members), f32),
        ],
    )(near(w), near(prods), *[near(x) for x in picked])


def joined(messages, members):
    slots = messages[0].shape[0] - members

    def join(*refs):
        ins, out = refs[:-1], refs[-1]
        total = ins[0][0:members]
        for r in ins[1:]:
            total = total + r[0:members]
        out[0:members] = total
        for i, r in enumerate(ins):
            out[members + i * slots : members + (i + 1) * slots] = r[members:]

    return call(
        join,
        out_shape=near_out((members + slots * len(messages), members), f32),
        in_specs=[VMEM] * len(messages),
        out_specs=VMEM,
    )(*[near(m) for m in messages])


def factor_inverse(groups):
    shape = groups[0].shape
    count = shape[0]
    x = list(groups)
    subl = lax.broadcasted_iota(jnp.int32, shape, 0)
    lane = lax.broadcasted_iota(jnp.int32, shape, 1)

    def wide(v, at):
        return jnp.broadcast_to(v[:, at : at + 1], shape)

    def tall(v, at):
        return jnp.broadcast_to(v[at : at + 1, :], shape)

    done = []
    for p, own in enumerate(x):
        base = p * count
        inside = (lane >= base) & (lane < base + count)
        column = [wide(own, base + j) for j in range(count)]
        s = {(i, j): tall(column[j], i) for j in range(count) for i in range(j, count)}
        row = jnp.where(inside, jnp.where(lane - base == subl, 1.0, 0.0), own)
        y = [tall(row, i) for i in range(count)]
        inv, low = [], {}
        for j in range(count):
            inv.append(1.0 / s[j, j])
            for i in range(j + 1, count):
                low[i, j] = s[i, j] * inv[j]
            for i in range(j + 1, count):
                for k in range(j + 1, i + 1):
                    s[i, k] = s[i, k] - (s[i, j] * s[k, j]) * inv[j]
            for i in range(j + 1, count):
                y[i] = y[i] - low[i, j] * y[j]
        out = jnp.zeros(shape, f32)
        for i in range(count):
            out = jnp.where(subl == i, y[i] * lax.rsqrt(s[i, i]), out)
        done.append(jnp.where(lane < base + count, out, 0.0))
        q = [None] * count
        for i in reversed(range(count)):
            q[i] = y[i] * inv[i]
            for k in range(i + 1, count):
                q[i] = q[i] - low[k, i] * q[k]
        for g in range(p + 1, len(x)):
            terms = [wide(x[g], base + t) * q[t] for t in range(count)]
            while len(terms) > 1:
                terms = [terms[t] + terms[t + 1] for t in range(0, len(terms), 2)]
            x[g] = jnp.where(inside, 0.0, x[g]) - terms[0]
    return done


def finish(message, y, decays, anomalies, place, slots, devices):
    members = message.shape[1]
    blocks, tile, _ = y.shape
    nodes = anomalies.shape[0]
    pieces = 8
    rows = nodes // pieces

    def analyse(place_ref, slot_ref, msg_ref, y_ref, a_ref, x_ref, w_ref, u_ref, left, right, gram, xs, us, ws, sems):
        load = [
            pltpu.make_async_copy(x_ref.at[pl.ds(i * rows, rows)], xs.at[pl.ds(i * rows, rows)], sems.at[i])
            for i in range(pieces)
        ]
        for c in load:
            c.start()
        place = place_ref[0]

        def one(d, c):
            slot = slot_ref[lax.bitwise_xor(d, place)]
            at = pl.multiple_of(members + slot * SLOT, SLOT)
            small = msg_ref[pl.ds(at, SLOT), :]
            v = small[1:2] + (0.5 * small[3:4]) * c
            left[pl.ds(d, 1), :] = v
            left[pl.ds(devices + d, 1), :] = c
            right[pl.ds(d, 1), :] = c
            right[pl.ds(devices + d, 1), :] = v
            return small[2:3] * c + small[0:1]

        lax.fori_loop(0, devices, one, jnp.zeros((1, members), f32))
        mine = right[pl.ds(place, 1), :]
        for j in range(blocks):
            ws[j] = y_ref[j] + a_ref[j] * mine
        store_w = pltpu.make_async_copy(ws, w_ref, sems.at[2 * pieces])
        store_w.start()
        r = lax.broadcasted_iota(jnp.int32, (members, members), 0)
        c = lax.broadcasted_iota(jnp.int32, (members, members), 1)
        gram[...] = (
            msg_ref[0:members]
            + lax.dot_general(
                left[...], right[...], (((0,), (0,)), ((), ())),
                precision=lax.Precision.HIGHEST, preferred_element_type=f32,
            )
            + jnp.where(r == c, members - 1.0, 0.0)
        )
        inverse = factor_inverse([gram[g : g + 8] for g in range(0, members, 8)])
        inverse = jnp.concatenate(inverse, axis=0) * math.sqrt(members - 1.0)
        transform = inverse.T.astype(bf16)
        store = []
        for i in range(pieces):
            at = pl.ds(i * rows, rows)
            load[i].wait()
            us[at, :] = jnp.dot(xs[at, :], transform, preferred_element_type=f32).astype(bf16)
            store.append(pltpu.make_async_copy(us.at[at], u_ref.at[at], sems.at[pieces + i]))
            store[i].start()
        store_w.wait()
        for c in store:
            c.wait()

    return call(
        analyse,
        out_shape=(
            jax.ShapeDtypeStruct(y.shape, f32),
            jax.ShapeDtypeStruct(anomalies.shape, bf16),
        ),
        in_specs=[SMEM, SMEM, VMEM, VMEM, VMEM, ANY],
        out_specs=(ANY, ANY),
        scratch_shapes=[pltpu.VMEM((2 * devices, members), f32)] * 2
        + [
            pltpu.VMEM((members, members), f32),
            pltpu.VMEM(anomalies.shape, bf16),
            pltpu.VMEM(anomalies.shape, bf16),
            pltpu.VMEM(y.shape, f32),
            pltpu.SemaphoreType.DMA((2 * pieces + 1,)),
        ],
    )(place, slots, near(message), near(y), near(decays), anomalies)


def local(anomalies, operator, local_tile_index, err_std, err_corr):
    members = anomalies.shape[1]
    tile = operator.shape[2]
    blocks = operator.shape[0]
    bands, regions = lax.axis_size("band"), lax.axis_size("region")
    devices = regions * bands
    place = (lax.axis_index("region") * bands + lax.axis_index("band")).astype(jnp.int32).reshape(1)
    tiles = anomalies.reshape(-1, tile, members)

    asked = [shifted(local_tile_index[:, k], "band", bands - k) for k in range(1, bands)]
    picked = [gather(tiles, local_tile_index[:, 0])]
    for k in range(1, bands):
        picked.append(shifted(gather(tiles, asked[k - 1]), "band", k))

    w, prods = weights(operator, err_std, err_corr)
    y, decays, message = whiten(w, prods, picked, 4)

    masks = [("band", list(range(1, bands)))]
    bit = 2
    while bit < regions:
        masks.append(("region", [bit, 2 * bit, 3 * bit] if 2 * bit < regions else [bit]))
        bit *= 4
    masks.append(("region", [1]))
    order = [0]
    for axis, group in masks:
        message = joined([message] + [swapped(message, axis, m) for m in group], members)
        unit = bands if axis == "region" else 1
        order = [o ^ (m * unit) for m in [0] + group for o in order]
    slots = jnp.array([order.index(t) for t in range(devices)], jnp.int32)

    whitened, updated = finish(message, y, decays, anomalies, place, slots, devices)
    return whitened.reshape(-1, members), updated


def solution(mesh):
    both = ("region", "band")
    placed = (P(both, None), P(both, None, None, None), P(both, None), P(both), P(both))
    return jax.shard_map(
        local, mesh=mesh, in_specs=placed, out_specs=(P(both, None), P(both, None)), check_vma=False
    )
```
